32 devices in a mesh: pb: 4 (over y, core), ka: 8 (over z, x).
Axes of the slice: x: 2, y: 2, z: 4, core: 2. Of those that a mesh axis runs over, the one named last changes fastest.
Arguments:
- queries: float32 [2048, 128], P('pb'), may hold values from -36 to 36
- cache_keys: float32 [65536, 128], P('ka'), may hold values from -4 to 4
- cache_values: float32 [65536, 128], P('ka'), may hold values from -6 to 6
- kept_index: int32 [4096], P('ka'), may hold values from 0 to 65535, as said below
Outputs:
- fitted: float32 [4096, 128], P('ka')
The draws below stay inside these ranges and needn't reach their ends.
Inputs may be any that keep to these rules, and one draw needn't show every extreme that they name: `kept_index`: Increasing; the t-th kept index lies among the cache rows t * (16) to (t + 1) * 16 - 1, so the kept keys of a device are rows of its own block of the cache.
All inputs are finite; a program needn't handle non-finite values.
Results may differ from the reference program's by a relative error of at most 0.0003.
Values sent between devices are 32-bit elements; how exact they have to be, the bound alone decides.
A program may use at most 128 MiB of HBM per device.

```python
import math
import jax
import jax.numpy as jnp
from jax import lax

HEAD = 128
KEEP_DEV = 512
CACHE_DEV = 8192
ITERS = 2
NQ = 2048
KEEP = 4096
CACHE = 65536


def kept_rows(key):
    stride = CACHE_DEV // KEEP_DEV
    offsets = jax.random.randint(jax.random.fold_in(key, 11), (KEEP,), 0, stride).astype(jnp.int32)
    offsets = offsets.at[0].set(0).at[KEEP - 1].set(stride - 1)
    positions = jnp.arange(KEEP, dtype=jnp.int32)
    return positions * stride + offsets


def draw_kept_index(key, part):
    return kept_rows(key).astype(jnp.int32)


def draw_cache_keys(key, part):
    drawn = jax.random.normal(jax.random.fold_in(key, 21), (CACHE, HEAD), jnp.float32)
    return jnp.clip(drawn, -4.0, 4.0)


def draw_queries(key, part):
    drawn = 3.0 * jax.random.normal(jax.random.fold_in(key, 31), (NQ, HEAD), jnp.float32)
    return jnp.clip(drawn, -36.0, 36.0)


def levels(key, dims, cuts, least, largest):
    factor_of, own = 1.0, jax.random.fold_in(key, 6)
    for dim, shards_of in cuts:
        heights = jnp.exp(jax.random.uniform(jax.random.fold_in(own, dim), (shards_of,), jnp.float32, least / len(cuts), largest / len(cuts)))
        factor_of = factor_of * jnp.repeat(heights, dims[dim] // shards_of).reshape([-1 if axis == dim else 1 for axis in range(len(dims))])
    return factor_of


def noise(rng, shape, deviation, limit, cuts=(), kind=jnp.bfloat16):
    result = jax.random.normal(rng, shape, jnp.float32) * deviation
    if len(cuts) > 0:
        result = levels(rng, shape, cuts, -0.22, 0.18) * result
    return jnp.clip(result, min=-limit, max=limit).astype(kind)


def setup_inputs(seed: int = 0) -> dict:
    splits = jax.random.split(jax.random.key(seed), 5)
    return {
        "queries": draw_queries(jax.random.fold_in(splits[4], 71), 0),
        "cache_keys": draw_cache_keys(jax.random.fold_in(splits[4], 71), 0),
        "cache_values": noise(splits[2], (CACHE, HEAD), 1.0, 6.0, ((0, 8),), jnp.float32),
        "kept_index": draw_kept_index(jax.random.fold_in(splits[4], 71), 0),
    }


ridge_weight = 0.01
highest = lax.Precision.HIGHEST

def softmax_rows(scores):
    top_row = lax.optimization_barrier(jnp.max(scores, axis=1, keepdims=True))
    exponent_rows = jnp.exp(scores - top_row)
    return exponent_rows / lax.optimization_barrier(jnp.sum(exponent_rows, axis=1, keepdims=True))

def reference(queries, cache_keys, cache_values, kept_index):
    inverse_root = 1.0 / math.sqrt(HEAD)
    block_rows = min(512, NQ)
    query_blocks = queries.reshape(NQ // block_rows, block_rows, HEAD)
    kept_keys = jnp.take(cache_keys, kept_index.astype(jnp.int32), axis=0)

    def target_block(query_rows):
        scores = jnp.dot(query_rows, cache_keys.T, precision=highest) * inverse_root
        return jnp.dot(softmax_rows(scores), cache_values, precision=highest)
    target = lax.map(target_block, query_blocks)

    def weights_of(query_rows):
        scores = jnp.dot(query_rows, kept_keys.T, precision=highest) * inverse_root
        return softmax_rows(scores)

    def project_back(rows_in):

        def add_block(running, block_pair):
            query_rows, side_rows = block_pair
            return (running + jnp.dot(weights_of(query_rows).T, side_rows, precision=highest), None)
        running, unused = lax.scan(add_block, jnp.zeros((KEEP, HEAD), jnp.float32), (query_blocks, rows_in))
        return running

    def forward(direction):
        return lax.map(lambda query_rows: jnp.dot(weights_of(query_rows), direction, precision=highest), query_blocks)
    residual = project_back(target)
    fitted = jnp.zeros((KEEP, HEAD), jnp.float32)
    direction = residual
    norm_now = lax.optimization_barrier(jnp.sum(residual * residual, axis=0))
    for iteration in range(ITERS):
        updates = forward(direction)
        operator_image = project_back(updates) + ridge_weight * direction
        step_length = norm_now / lax.optimization_barrier(jnp.sum(direction * operator_image, axis=0))
        fitted = fitted + step_length * direction
        if iteration + 1 < ITERS:
            residual = residual - step_length * operator_image
            norm_next = lax.optimization_barrier(jnp.sum(residual * residual, axis=0))
            direction = residual + norm_next / norm_now * direction
            norm_now = norm_next
    return fitted
```

```python
import math

import jax
import jax.numpy as jnp
from jax import lax
from jax.sharding import PartitionSpec as P

ITERS = 2


ridge_weight = 0.01
highest = lax.Precision.HIGHEST


def contract(left_side, right_side, left_dim, right_dim):
    return lax.dot_general(
        left_side,
        right_side,
        (((left_dim,), (right_dim,)), ((), ())),
        precision=highest,
        preferred_element_type=jnp.float32,
    )


def column_sums(left_side, right_side):
    return jnp.sum(left_side * right_side, axis=0, keepdims=True)


def padded(rows, *tail):
    used = sum(part.shape[0] for part in tail)
    fill = jnp.zeros((-used % 8, rows.shape[1]), rows.dtype)
    return jnp.concatenate((rows,) + tail + (fill,), axis=0)


def shards(queries, cache_keys, cache_values, kept_index):
    query_rows, head_width = queries.shape
    inverse_root = 1.0 / math.sqrt(head_width)
    cache_rows = cache_keys.shape[0]
    block_size = min(1024, cache_rows)
    blocks = cache_rows // block_size

    local_kept = kept_index - lax.axis_index("ka") * cache_rows
    kept_keys = jnp.take(cache_keys, local_kept, axis=0)
    kept_scores = contract(queries, kept_keys, 1, 1) * inverse_root
    kept_top = jnp.max(kept_scores, axis=1)
    kept_exponent = jnp.exp(kept_scores - kept_top[:, None])
    kept_total = jnp.sum(kept_exponent, axis=1)

    def step(block_number, state):
        top, total, numerator = state
        start = block_number * block_size
        keys_block = lax.dynamic_slice_in_dim(cache_keys, start, block_size, axis=0)
        values_block = lax.dynamic_slice_in_dim(cache_values, start, block_size, axis=0)
        scores = contract(queries, keys_block, 1, 1) * inverse_root
        top_next = jnp.maximum(top, jnp.max(scores, axis=1))
        factor = jnp.exp(top - top_next)
        exponent = jnp.exp(scores - top_next[:, None])
        return (
            top_next,
            total * factor + jnp.sum(exponent, axis=1),
            numerator * factor[:, None] + contract(exponent, values_block, 1, 0),
        )

    top, total, numerator = lax.fori_loop(
        0,
        blocks,
        step,
        (
            jnp.full((query_rows,), -jnp.inf, jnp.float32),
            jnp.zeros((query_rows,), jnp.float32),
            jnp.zeros((query_rows, head_width), jnp.float32),
        ),
    )

    stats = jnp.concatenate((top, total, kept_top, kept_total)).reshape(-1, head_width)
    gathered = lax.all_gather(padded(numerator, stats), "ka")
    shares = gathered.shape[0]
    gathered_stats = gathered[:, query_rows : query_rows + stats.shape[0]]
    gathered_stats = gathered_stats.reshape(shares, 4, query_rows)
    factors = jnp.exp(gathered_stats[:, 0] - jnp.max(gathered_stats[:, 0], axis=0))
    target_total = jnp.sum(gathered_stats[:, 1] * factors, axis=0)
    target = jnp.sum(gathered[:, :query_rows] * factors[:, :, None], axis=0)
    target = target / target_total[:, None]
    kept_joint = jnp.max(gathered_stats[:, 2], axis=0)
    joint_total = jnp.sum(gathered_stats[:, 3] * jnp.exp(gathered_stats[:, 2] - kept_joint), axis=0)
    weights = kept_exponent * (jnp.exp(kept_top - kept_joint) / joint_total)[:, None]

    residual = lax.psum(contract(weights, target, 0, 0), "pb")
    kept_rows = residual.shape[0]
    fitted = jnp.zeros_like(residual)
    direction = residual
    updates = None
    norm_now = None
    length_now = None
    for iteration in range(ITERS):
        final_turn = iteration + 1 == ITERS
        forward = contract(weights, residual, 1, 0)
        if iteration == 0:
            summed = lax.psum(padded(forward, column_sums(residual, residual)), "ka")
            updates = summed[:query_rows]
            norm_now = summed[query_rows : query_rows + 1]
            length_now = norm_now
        else:
            summed = lax.psum(
                padded(
                    forward,
                    column_sums(residual, residual),
                    column_sums(residual, direction),
                ),
                "ka",
            )
            norm_next = summed[query_rows : query_rows + 1]
            crossed = summed[query_rows + 1 : query_rows + 2]
            ratio = norm_next / norm_now
            direction = residual + ratio * direction
            updates = summed[:query_rows] + ratio * updates
            length_now = norm_next + 2.0 * ratio * crossed + ratio * ratio * length_now
            norm_now = norm_next
        energy = column_sums(updates, updates)
        if final_turn:
            energy = lax.psum(energy, "pb")
            fitted = fitted + norm_now / (energy + ridge_weight * length_now) * direction
        else:
            summed = lax.psum(padded(contract(weights, updates, 0, 0), energy), "pb")
            operator_image = summed[:kept_rows] + ridge_weight * direction
            energy = summed[kept_rows : kept_rows + 1]
            step_length = norm_now / (energy + ridge_weight * length_now)
            fitted = fitted + step_length * direction
            residual = residual - step_length * operator_image
    return fitted


def solution(mesh):
    in_specs = (P("pb", None), P("ka", None), P("ka", None), P("ka"))
    out_specs = P("ka", None)
    return jax.shard_map(shards, mesh=mesh, in_specs=in_specs, out_specs=out_specs, check_vma=False)
```

```python
import functools
import math

import jax
import jax.numpy as jnp
from jax import lax
from jax.experimental import pallas as pl
from jax.experimental.pallas import tpu as pltpu
from jax.sharding import PartitionSpec as P

ITERS = 2


ridge_weight = 0.01
highest = lax.Precision.HIGHEST


def contract(left_side, right_side, left_dim, right_dim):
    return lax.dot_general(
        left_side,
        right_side,
        (((left_dim,), (right_dim,)), ((), ())),
        precision=highest,
        preferred_element_type=jnp.float32,
    )


def column_sums(left_side, right_side):
    return jnp.sum(left_side * right_side, axis=0, keepdims=True)


def fit_kernel(
    ka_size,
    pb_size,
    part_ref,
    kept_ref,
    fitted_ref,
    flipped,
    stats_in,
    stats_all,
    ka_out,
    ka_in,
    ka_all,
    pb_out,
    pb_in,
    pb_all,
    tail_out,
    tail_in,
    ka_send,
    ka_recv,
    pb_send,
    pb_recv,
):
    ka_me = lax.axis_index("ka")
    pb_me = lax.axis_index("pb")
    width = fitted_ref.shape[1]
    query_rows = kept_ref.shape[0]
    kept_rows = kept_ref.shape[1]
    ka_share = query_rows // ka_size
    pb_share = kept_rows // pb_size

    def peer_of(axis, offset):
        size = ka_size if axis == "ka" else pb_size
        me = ka_me if axis == "ka" else pb_me
        return lax.rem(me + offset, size)

    barrier = pltpu.get_barrier_semaphore()
    for axis, size in (("ka", ka_size), ("pb", pb_size)):
        for offset in range(1, size):
            pl.semaphore_signal(
                barrier,
                inc=1,
                device_id={axis: peer_of(axis, offset)},
                device_id_type=pl.DeviceIdType.MESH,
            )
    pl.semaphore_wait(barrier, ka_size + pb_size - 2)

    def begin(axis, phase, source_of, target):
        size, send, recv = (
            (ka_size, ka_send, ka_recv) if axis == "ka" else (pb_size, pb_send, pb_recv)
        )
        copies = []
        for offset in range(1, size):
            peer = peer_of(axis, offset)
            copy = pltpu.make_async_remote_copy(
                src_ref=source_of(peer),
                dst_ref=target,
                send_sem=send.at[phase, offset],
                recv_sem=recv.at[phase, offset],
                device_id={axis: peer},
                device_id_type=pl.DeviceIdType.MESH,
            )
            copy.start()
            copies.append(copy)
        return copies

    def finish(copies):
        for copy in copies:
            copy.wait()

    def scattered_sum(axis, phase, value, tail, out, arrived, whole):
        me, size, share = (
            (ka_me, ka_size, ka_share) if axis == "ka" else (pb_me, pb_size, pb_share)
        )
        out[:, :share, :] = value.reshape(size, share, width)
        out[:, share:, :] = jnp.broadcast_to(tail[None], (size, 8, width))
        copies = begin(axis, phase, lambda peer: out.at[peer], arrived.at[me])
        arrived[me] = out[me]
        finish(copies)
        total = arrived[0]
        for source in range(1, size):
            total = total + arrived[source]
        whole[me] = total[:share]
        finish(begin(axis, phase + 1, lambda peer: whole.at[me], whole.at[me]))
        return whole[...].reshape(size * share, width), total[share:]

    def matmul(left_side, right_side):
        return jnp.dot(
            left_side, right_side, precision=highest, preferred_element_type=jnp.float32
        )

    def tail_rows(*rows):
        place = lax.broadcasted_iota(jnp.int32, (8, width), 0)
        tail = jnp.zeros((8, width), jnp.float32)
        for number, row in enumerate(rows):
            tail = jnp.where(place == number, row, tail)
        return tail

    copies = begin("ka", 0, lambda peer: part_ref.at[peer], stats_in.at[ka_me])
    stats_in[ka_me] = part_ref[ka_me]
    flipped[...] = kept_ref[...].T
    finish(copies)

    def column(source, number):
        return stats_in[source, :, width + number : width + number + 1]

    top = column(0, 0)
    kept_top = column(0, 2)
    for source in range(1, ka_size):
        top = jnp.maximum(top, column(source, 0))
        kept_top = jnp.maximum(kept_top, column(source, 2))
    total = jnp.zeros_like(top)
    kept_total = jnp.zeros_like(top)
    numerator = jnp.zeros((ka_share, width), jnp.float32)
    for source in range(ka_size):
        factor = jnp.exp(column(source, 0) - top)
        total = total + column(source, 1) * factor
        numerator = numerator + stats_in[source, :, :width] * factor
        kept_total = kept_total + column(source, 3) * jnp.exp(column(source, 2) - kept_top)
    lane = lax.broadcasted_iota(jnp.int32, (ka_share, width), 1)
    stats_all[ka_me, :, :width] = numerator / total
    stats_all[ka_me, :, width:] = jnp.where(lane == 0, kept_top, kept_total)
    finish(begin("ka", 1, lambda peer: stats_all.at[ka_me], stats_all.at[ka_me]))
    target = stats_all[:, :, :width].reshape(query_rows, width)
    joint_top = stats_all[:, :, width : width + 1].reshape(query_rows, 1)
    joint_total = stats_all[:, :, width + 1 : width + 2].reshape(query_rows, 1)
    own_top = part_ref[:, :, width + 2 : width + 3].reshape(query_rows, 1)
    scale = jnp.exp(own_top - joint_top) / joint_total

    no_tail = jnp.zeros((8, width), jnp.float32)
    residual, _ = scattered_sum(
        "pb",
        0,
        matmul(flipped[...], scale * target),
        no_tail,
        pb_out.at[0],
        pb_in.at[0],
        pb_all.at[0],
    )
    fitted = jnp.zeros_like(residual)
    direction = residual
    updates = None
    norm_now = None
    length_now = None
    for iteration in range(ITERS):
        forward = scale * matmul(kept_ref[...], residual)
        tail = tail_rows(column_sums(residual, residual), column_sums(residual, direction))
        summed, tail = scattered_sum(
            "ka",
            2 + 2 * iteration,
            forward,
            tail,
            ka_out.at[iteration],
            ka_in.at[iteration],
            ka_all.at[iteration],
        )
        norm_next = tail[0:1]
        if iteration == 0:
            updates = summed
            length_now = norm_next
        else:
            ratio = norm_next / norm_now
            direction = residual + ratio * direction
            updates = summed + ratio * updates
            length_now = norm_next + 2.0 * ratio * tail[1:2] + ratio * ratio * length_now
        norm_now = norm_next
        energy = tail_rows(column_sums(updates, updates))
        if iteration + 1 == ITERS:
            tail_out[...] = energy
            copies = begin("pb", 2 * ITERS, lambda peer: tail_out, tail_in.at[pb_me])
            tail_in[pb_me] = energy
            finish(copies)
            energy = tail_in[0]
            for source in range(1, pb_size):
                energy = energy + tail_in[source]
            step_length = norm_now / (energy[0:1] + ridge_weight * length_now)
            fitted_ref[...] = fitted + step_length * direction
        else:
            image, energy = scattered_sum(
                "pb",
                2 + 2 * iteration,
                matmul(flipped[...], scale * updates),
                energy,
                pb_out.at[iteration + 1],
                pb_in.at[iteration + 1],
                pb_all.at[iteration + 1],
            )
            step_length = norm_now / (energy[0:1] + ridge_weight * length_now)
            fitted = fitted + step_length * direction
            residual = residual - step_length * (image + ridge_weight * direction)


def fit(part, kept_exponent):
    ka_size, pb_size = lax.axis_size("ka"), lax.axis_size("pb")
    query_rows, kept_rows = kept_exponent.shape
    width = part.shape[1] // 2
    ka_share, pb_share = query_rows // ka_size, kept_rows // pb_size
    space = functools.partial(pltpu.VMEM, dtype=jnp.float32)
    return pl.pallas_call(
        functools.partial(fit_kernel, ka_size, pb_size),
        out_shape=jax.ShapeDtypeStruct((kept_rows, width), jnp.float32),
        in_specs=[pl.BlockSpec(memory_space=pltpu.VMEM)] * 2,
        out_specs=pl.BlockSpec(memory_space=pltpu.VMEM),
        scratch_shapes=[
            space((kept_rows, query_rows)),
            space((ka_size, ka_share, 2 * width)),
            space((ka_size, ka_share, 2 * width)),
            space((ITERS, ka_size, ka_share + 8, width)),
            space((ITERS, ka_size, ka_share + 8, width)),
            space((ITERS, ka_size, ka_share, width)),
            space((ITERS, pb_size, pb_share + 8, width)),
            space((ITERS, pb_size, pb_share + 8, width)),
            space((ITERS, pb_size, pb_share, width)),
            space((8, width)),
            space((pb_size, 8, width)),
            pltpu.SemaphoreType.DMA((2 + 2 * ITERS, ka_size)),
            pltpu.SemaphoreType.DMA((2 + 2 * ITERS, ka_size)),
            pltpu.SemaphoreType.DMA((2 * ITERS + 1, pb_size)),
            pltpu.SemaphoreType.DMA((2 * ITERS + 1, pb_size)),
        ],
        compiler_params=pltpu.CompilerParams(
            collective_id=0, has_side_effects=True, vmem_limit_bytes=40 * 1024 * 1024
        ),
    )(part.reshape(ka_size, ka_share, 2 * width), kept_exponent)


def shards(queries, cache_keys, cache_values, kept_index):
    query_rows, head_width = queries.shape
    inverse_root = 1.0 / math.sqrt(head_width)
    cache_rows = cache_keys.shape[0]
    block_size = min(1024, cache_rows)
    blocks = cache_rows // block_size

    local_kept = kept_index - lax.axis_index("ka") * cache_rows
    kept_keys = jnp.take(cache_keys, local_kept, axis=0)
    kept_scores = contract(queries, kept_keys, 1, 1) * inverse_root
    kept_top = jnp.max(kept_scores, axis=1)
    kept_exponent = jnp.exp(kept_scores - kept_top[:, None])
    kept_total = jnp.sum(kept_exponent, axis=1)

    def step(block_number, state):
        top, total, numerator = state
        start = block_number * block_size
        keys_block = lax.dynamic_slice_in_dim(cache_keys, start, block_size, axis=0)
        values_block = lax.dynamic_slice_in_dim(cache_values, start, block_size, axis=0)
        scores = contract(queries, keys_block, 1, 1) * inverse_root
        top_next = jnp.maximum(top, jnp.max(scores, axis=1))
        factor = jnp.exp(top - top_next)
        exponent = jnp.exp(scores - top_next[:, None])
        return (
            top_next,
            total * factor + jnp.sum(exponent, axis=1),
            numerator * factor[:, None] + contract(exponent, values_block, 1, 0),
        )

    top, total, numerator = lax.fori_loop(
        0,
        blocks,
        step,
        (
            jnp.full((query_rows,), -jnp.inf, jnp.float32),
            jnp.zeros((query_rows,), jnp.float32),
            jnp.zeros((query_rows, head_width), jnp.float32),
        ),
    )

    stats = jnp.stack((top, total, kept_top, kept_total), axis=1)
    stats = jnp.pad(stats, ((0, 0), (0, head_width - 4)))
    return fit(jnp.concatenate((numerator, stats), axis=1), kept_exponent)


def solution(mesh):
    in_specs = (P("pb", None), P("ka", None), P("ka", None), P("ka"))
    out_specs = P("ka", None)
    return jax.shard_map(shards, mesh=mesh, in_specs=in_specs, out_specs=out_specs, check_vma=False)
```

```python
import functools
import math

import jax
import jax.numpy as jnp
from jax import lax
from jax.experimental import pallas as pl
from jax.experimental.pallas import tpu as pltpu
from jax.sharding import PartitionSpec as P

ITERS = 2


ridge_weight = 0.01
highest = lax.Precision.HIGHEST


def contract(left_side, right_side, left_dim, right_dim):
    return lax.dot_general(
        left_side,
        right_side,
        (((left_dim,), (right_dim,)), ((), ())),
        precision=highest,
        preferred_element_type=jnp.float32,
    )


def column_sums(left_side, right_side):
    return jnp.sum(left_side * right_side, axis=0, keepdims=True)


def fit_kernel(
    ka_size,
    pb_size,
    part_ref,
    kept_ref,
    fitted_ref,
    flipped,
    stats_in,
    stats_all,
    ka_out,
    ka_in,
    ka_all,
    pb_out,
    pb_in,
    pb_all,
    tail_out,
    tail_in,
    ka_send,
    ka_recv,
    pb_send,
    pb_recv,
):
    ka_me = lax.axis_index("ka")
    pb_me = lax.axis_index("pb")
    width = fitted_ref.shape[1]
    query_rows = kept_ref.shape[0]
    kept_rows = kept_ref.shape[1]
    ka_share = query_rows // ka_size
    pb_share = kept_rows // pb_size

    def peer_of(axis, offset):
        size = ka_size if axis == "ka" else pb_size
        me = ka_me if axis == "ka" else pb_me
        return lax.rem(me + offset, size)

    barrier = pltpu.get_barrier_semaphore()
    for axis, size in (("ka", ka_size), ("pb", pb_size)):
        for offset in range(1, size):
            pl.semaphore_signal(
                barrier,
                inc=1,
                device_id={axis: peer_of(axis, offset)},
                device_id_type=pl.DeviceIdType.MESH,
            )
    pl.semaphore_wait(barrier, ka_size + pb_size - 2)

    def begin(axis, phase, source_of, target):
        size, send, recv = (
            (ka_size, ka_send, ka_recv) if axis == "ka" else (pb_size, pb_send, pb_recv)
        )
        copies = []
        for offset in range(1, size):
            peer = peer_of(axis, offset)
            copy = pltpu.make_async_remote_copy(
                src_ref=source_of(peer),
                dst_ref=target,
                send_sem=send.at[phase, offset],
                recv_sem=recv.at[phase, offset],
                device_id={axis: peer},
                device_id_type=pl.DeviceIdType.MESH,
            )
            copy.start()
            copies.append(copy)
        return copies

    def finish(copies):
        for copy in copies:
            copy.wait()

    def scattered_sum(axis, phase, value, tail, out, arrived, whole):
        me, size, share = (
            (ka_me, ka_size, ka_share) if axis == "ka" else (pb_me, pb_size, pb_share)
        )
        out[:, :share, :] = value.reshape(size, share, width)
        out[:, share:, :] = jnp.broadcast_to(tail[None], (size, 8, width))
        copies = begin(axis, phase, lambda peer: out.at[peer], arrived.at[me])
        arrived[me] = out[me]
        finish(copies)
        total = arrived[0]
        for source in range(1, size):
            total = total + arrived[source]
        whole[me] = total[:share]
        finish(begin(axis, phase + 1, lambda peer: whole.at[me], whole.at[me]))
        return whole[...].reshape(size * share, width), total[share:]

    def matmul(left_side, right_side):
        return jnp.dot(
            left_side, right_side, precision=highest, preferred_element_type=jnp.float32
        )

    def tail_rows(*rows):
        place = lax.broadcasted_iota(jnp.int32, (8, width), 0)
        tail = jnp.zeros((8, width), jnp.float32)
        for number, row in enumerate(rows):
            tail = jnp.where(place == number, row, tail)
        return tail

    copies = begin("ka", 0, lambda peer: part_ref.at[peer], stats_in.at[ka_me])
    stats_in[ka_me] = part_ref[ka_me]
    flipped[...] = kept_ref[...].T
    finish(copies)

    def column(source, number):
        return stats_in[source, :, width + number : width + number + 1]

    top = column(0, 0)
    kept_top = column(0, 2)
    for source in range(1, ka_size):
        top = jnp.maximum(top, column(source, 0))
        kept_top = jnp.maximum(kept_top, column(source, 2))
    total = jnp.zeros_like(top)
    kept_total = jnp.zeros_like(top)
    numerator = jnp.zeros((ka_share, width), jnp.float32)
    for source in range(ka_size):
        factor = jnp.exp(column(source, 0) - top)
        total = total + column(source, 1) * factor
        numerator = numerator + stats_in[source, :, :width] * factor
        kept_total = kept_total + column(source, 3) * jnp.exp(column(source, 2) - kept_top)
    lane = lax.broadcasted_iota(jnp.int32, (ka_share, width), 1)
    stats_all[ka_me, :, :width] = numerator / total
    stats_all[ka_me, :, width:] = jnp.where(lane == 0, kept_top, kept_total)
    finish(begin("ka", 1, lambda peer: stats_all.at[ka_me], stats_all.at[ka_me]))
    target = stats_all[:, :, :width].reshape(query_rows, width)
    joint_top = stats_all[:, :, width : width + 1].reshape(query_rows, 1)
    joint_total = stats_all[:, :, width + 1 : width + 2].reshape(query_rows, 1)
    own_top = part_ref[:, :, width + 2 : width + 3].reshape(query_rows, 1)
    scale = jnp.exp(own_top - joint_top) / joint_total

    no_tail = jnp.zeros((8, width), jnp.float32)
    residual, _ = scattered_sum(
        "pb",
        0,
        matmul(flipped[...], scale * target),
        no_tail,
        pb_out.at[0],
        pb_in.at[0],
        pb_all.at[0],
    )
    fitted = jnp.zeros_like(residual)
    direction = residual
    updates = None
    norm_now = None
    length_now = None
    for iteration in range(ITERS):
        forward = scale * matmul(kept_ref[...], residual)
        tail = tail_rows(column_sums(residual, residual), column_sums(residual, direction))
        summed, tail = scattered_sum(
            "ka",
            2 + 2 * iteration,
            forward,
            tail,
            ka_out.at[iteration],
            ka_in.at[iteration],
            ka_all.at[iteration],
        )
        norm_next = tail[0:1]
        if iteration == 0:
            updates = summed
            length_now = norm_next
        else:
            ratio = norm_next / norm_now
            direction = residual + ratio * direction
            updates = summed + ratio * updates
            length_now = norm_next + 2.0 * ratio * tail[1:2] + ratio * ratio * length_now
        norm_now = norm_next
        energy = tail_rows(column_sums(updates, updates))
        if iteration + 1 == ITERS:
            tail_out[...] = energy
            copies = begin("pb", 2 * ITERS, lambda peer: tail_out, tail_in.at[pb_me])
            tail_in[pb_me] = energy
            finish(copies)
            energy = tail_in[0]
            for source in range(1, pb_size):
                energy = energy + tail_in[source]
            step_length = norm_now / (energy[0:1] + ridge_weight * length_now)
            fitted_ref[...] = fitted + step_length * direction
        else:
            image, energy = scattered_sum(
                "pb",
                2 + 2 * iteration,
                matmul(flipped[...], scale * updates),
                energy,
                pb_out.at[iteration + 1],
                pb_in.at[iteration + 1],
                pb_all.at[iteration + 1],
            )
            step_length = norm_now / (energy[0:1] + ridge_weight * length_now)
            fitted = fitted + step_length * direction
            residual = residual - step_length * (image + ridge_weight * direction)


def fit(part, kept_exponent):
    ka_size, pb_size = lax.axis_size("ka"), lax.axis_size("pb")
    query_rows, kept_rows = kept_exponent.shape
    width = part.shape[1] // 2
    ka_share, pb_share = query_rows // ka_size, kept_rows // pb_size
    space = functools.partial(pltpu.VMEM, dtype=jnp.float32)
    return pl.pallas_call(
        functools.partial(fit_kernel, ka_size, pb_size),
        out_shape=jax.ShapeDtypeStruct((kept_rows, width), jnp.float32),
        in_specs=[pl.BlockSpec(memory_space=pltpu.VMEM)] * 2,
        out_specs=pl.BlockSpec(memory_space=pltpu.VMEM),
        scratch_shapes=[
            space((kept_rows, query_rows)),
            space((ka_size, ka_share, 2 * width)),
            space((ka_size, ka_share, 2 * width)),
            space((ITERS, ka_size, ka_share + 8, width)),
            space((ITERS, ka_size, ka_share + 8, width)),
            space((ITERS, ka_size, ka_share, width)),
            space((ITERS, pb_size, pb_share + 8, width)),
            space((ITERS, pb_size, pb_share + 8, width)),
            space((ITERS, pb_size, pb_share, width)),
            space((8, width)),
            space((pb_size, 8, width)),
            pltpu.SemaphoreType.DMA((2 + 2 * ITERS, ka_size)),
            pltpu.SemaphoreType.DMA((2 + 2 * ITERS, ka_size)),
            pltpu.SemaphoreType.DMA((2 * ITERS + 1, pb_size)),
            pltpu.SemaphoreType.DMA((2 * ITERS + 1, pb_size)),
        ],
        compiler_params=pltpu.CompilerParams(
            collective_id=0, has_side_effects=True, vmem_limit_bytes=40 * 1024 * 1024
        ),
    )(part.reshape(ka_size, ka_share, 2 * width), kept_exponent)


def thirds(value):
    first = value.astype(jnp.bfloat16)
    rest = value - first.astype(jnp.float32)
    second = rest.astype(jnp.bfloat16)
    third = (rest - second.astype(jnp.float32)).astype(jnp.bfloat16)
    return first, second, third


def target_kernel(inverse_root, queries_ref, keys_ref, values_ref, kept_ref, part_ref, wide, top, total, sums):
    width = queries_ref.shape[1]

    @pl.when(pl.program_id(0) == 0)
    def _():
        one, two, three = thirds(queries_ref[...])
        wide[...] = jnp.concatenate((one, one, two, one, three, two), axis=1)
        top[...] = jnp.full_like(top, -jnp.inf)
        total[...] = jnp.zeros_like(total)
        sums[...] = jnp.zeros_like(sums)

    one, two, three = thirds(keys_ref[...])
    scores = (
        lax.dot_general(
            wide[...],
            jnp.concatenate((one, two, one, three, one, two), axis=1),
            (((1,), (1,)), ((), ())),
            preferred_element_type=jnp.float32,
        )
        * inverse_root
    )
    top_next = jnp.maximum(top[...], jnp.max(scores, axis=1, keepdims=True))
    factor = jnp.exp(top[...] - top_next)
    exponent = jnp.exp(scores - top_next)
    top[...] = top_next
    total[...] = total[...] * factor + jnp.sum(exponent, axis=1, keepdims=True)
    one, two, three = thirds(values_ref[...])
    high, middle, low = thirds(exponent)
    pair = jnp.concatenate((one, two), axis=1)
    product = functools.partial(jnp.dot, preferred_element_type=jnp.float32)
    both = product(high, pair) + product(middle, pair)
    small = product(high, three) + product(low, one)
    sums[...] = sums[...] * factor + (both[:, :width] + (both[:, width:] + small))

    @pl.when(pl.program_id(0) == pl.num_programs(0) - 1)
    def _():
        lane = lax.broadcasted_iota(jnp.int32, kept_ref.shape, 1)
        stats = jnp.where(lane == 0, top[...], jnp.where(lane == 1, total[...], kept_ref[...]))
        part_ref[:, :width] = sums[...]
        part_ref[:, width:] = stats


def target_part(queries, cache_keys, cache_values, kept_stats, inverse_root):
    query_rows, width = queries.shape
    block_size = min(1024, cache_keys.shape[0])
    fixed = pl.BlockSpec((query_rows, width), lambda block: (0, 0))
    moving = pl.BlockSpec((block_size, width), lambda block: (block, 0))
    return pl.pallas_call(
        functools.partial(target_kernel, inverse_root),
        grid=(cache_keys.shape[0] // block_size,),
        out_shape=jax.ShapeDtypeStruct((query_rows, 2 * width), jnp.float32),
        in_specs=[fixed, moving, moving, fixed],
        out_specs=pl.BlockSpec((query_rows, 2 * width), lambda block: (0, 0)),
        scratch_shapes=[
            pltpu.VMEM((query_rows, 6 * width), jnp.bfloat16),
            pltpu.VMEM((query_rows, 1), jnp.float32),
            pltpu.VMEM((query_rows, 1), jnp.float32),
            pltpu.VMEM((query_rows, width), jnp.float32),
        ],
        compiler_params=pltpu.CompilerParams(vmem_limit_bytes=40 * 1024 * 1024),
    )(queries, cache_keys, cache_values, kept_stats)


def shards(queries, cache_keys, cache_values, kept_index):
    head_width = queries.shape[1]
    inverse_root = 1.0 / math.sqrt(head_width)
    cache_rows = cache_keys.shape[0]

    local_kept = kept_index - lax.axis_index("ka") * cache_rows
    kept_keys = jnp.take(cache_keys, local_kept, axis=0)
    kept_scores = contract(queries, kept_keys, 1, 1) * inverse_root
    kept_top = jnp.max(kept_scores, axis=1)
    kept_exponent = jnp.exp(kept_scores - kept_top[:, None])
    kept_total = jnp.sum(kept_exponent, axis=1)

    zero = jnp.zeros_like(kept_top)
    stats = jnp.stack((zero, zero, kept_top, kept_total), axis=1)
    stats = jnp.pad(stats, ((0, 0), (0, head_width - 4)))
    return fit(
        target_part(queries, cache_keys, cache_values, stats, inverse_root), kept_exponent
    )


def solution(mesh):
    in_specs = (P("pb", None), P("ka", None), P("ka", None), P("ka"))
    out_specs = P("ka", None)
    return jax.shard_map(shards, mesh=mesh, in_specs=in_specs, out_specs=out_specs, check_vma=False)
```

```python
import functools
import math

import jax
import jax.numpy as jnp
from jax import lax
from jax.experimental import pallas as pl
from jax.experimental.pallas import tpu as pltpu
from jax.sharding import PartitionSpec as P

ITERS = 2


ridge_weight = 0.01
highest = lax.Precision.HIGHEST


def contract(left_side, right_side, left_dim, right_dim):
    return lax.dot_general(
        left_side,
        right_side,
        (((left_dim,), (right_dim,)), ((), ())),
        precision=highest,
        preferred_element_type=jnp.float32,
    )


def column_sums(left_side, right_side):
    return jnp.sum(left_side * right_side, axis=0, keepdims=True)


def fit_kernel(
    ka_size,
    pb_size,
    part_ref,
    kept_ref,
    fitted_ref,
    flipped,
    stats_in,
    stats_all,
    ka_out,
    ka_in,
    ka_all,
    pb_out,
    pb_in,
    pb_all,
    tail_out,
    tail_in,
    ka_send,
    ka_recv,
    pb_send,
    pb_recv,
):
    ka_me = lax.axis_index("ka")
    pb_me = lax.axis_index("pb")
    width = fitted_ref.shape[1]
    query_rows = kept_ref.shape[0]
    kept_rows = kept_ref.shape[1]
    ka_share = query_rows // ka_size
    pb_share = kept_rows // pb_size

    def peer_of(axis, offset):
        size = ka_size if axis == "ka" else pb_size
        me = ka_me if axis == "ka" else pb_me
        return lax.rem(me + offset, size)

    barrier = pltpu.get_barrier_semaphore()
    for axis, size in (("ka", ka_size), ("pb", pb_size)):
        for offset in range(1, size):
            pl.semaphore_signal(
                barrier,
                inc=1,
                device_id={axis: peer_of(axis, offset)},
                device_id_type=pl.DeviceIdType.MESH,
            )
    pl.semaphore_wait(barrier, ka_size + pb_size - 2)

    def begin(axis, phase, source_of, target):
        size, send, recv = (
            (ka_size, ka_send, ka_recv) if axis == "ka" else (pb_size, pb_send, pb_recv)
        )
        copies = []
        for offset in range(1, size):
            peer = peer_of(axis, offset)
            copy = pltpu.make_async_remote_copy(
                src_ref=source_of(peer),
                dst_ref=target,
                send_sem=send.at[phase, offset],
                recv_sem=recv.at[phase, offset],
                device_id={axis: peer},
                device_id_type=pl.DeviceIdType.MESH,
            )
            copy.start()
            copies.append(copy)
        return copies

    def finish(copies):
        for copy in copies:
            copy.wait()

    def scattered_sum(axis, phase, value, tail, out, arrived, whole):
        me, size, share = (
            (ka_me, ka_size, ka_share) if axis == "ka" else (pb_me, pb_size, pb_share)
        )
        out[:, :share, :] = value.reshape(size, share, width)
        out[:, share:, :] = jnp.broadcast_to(tail[None], (size, 8, width))
        copies = begin(axis, phase, lambda peer: out.at[peer], arrived.at[me])
        arrived[me] = out[me]
        finish(copies)
        total = arrived[0]
        for source in range(1, size):
            total = total + arrived[source]
        whole[me] = total[:share]
        finish(begin(axis, phase + 1, lambda peer: whole.at[me], whole.at[me]))
        return whole[...].reshape(size * share, width), total[share:]

    def matmul(left_side, right_side):
        return jnp.dot(
            left_side, right_side, precision=highest, preferred_element_type=jnp.float32
        )

    def tail_rows(*rows):
        place = lax.broadcasted_iota(jnp.int32, (8, width), 0)
        tail = jnp.zeros((8, width), jnp.float32)
        for number, row in enumerate(rows):
            tail = jnp.where(place == number, row, tail)
        return tail

    copies = begin("ka", 0, lambda peer: part_ref.at[peer], stats_in.at[ka_me])
    stats_in[ka_me] = part_ref[ka_me]
    flipped[...] = kept_ref[...].T
    finish(copies)

    def column(source, number):
        return stats_in[source, :, width + number : width + number + 1]

    top = column(0, 0)
    kept_top = column(0, 2)
    for source in range(1, ka_size):
        top = jnp.maximum(top, column(source, 0))
        kept_top = jnp.maximum(kept_top, column(source, 2))
    total = jnp.zeros_like(top)
    kept_total = jnp.zeros_like(top)
    numerator = jnp.zeros((ka_share, width), jnp.float32)
    for source in range(ka_size):
        factor = jnp.exp(column(source, 0) - top)
        total = total + column(source, 1) * factor
        numerator = numerator + stats_in[source, :, :width] * factor
        kept_total = kept_total + column(source, 3) * jnp.exp(column(source, 2) - kept_top)
    lane = lax.broadcasted_iota(jnp.int32, (ka_share, width), 1)
    stats_all[ka_me, :, :width] = numerator / total
    stats_all[ka_me, :, width:] = jnp.where(lane == 0, kept_top, kept_total)
    finish(begin("ka", 1, lambda peer: stats_all.at[ka_me], stats_all.at[ka_me]))
    target = stats_all[:, :, :width].reshape(query_rows, width)
    joint_top = stats_all[:, :, width : width + 1].reshape(query_rows, 1)
    joint_total = stats_all[:, :, width + 1 : width + 2].reshape(query_rows, 1)
    own_top = part_ref[:, :, width + 2 : width + 3].reshape(query_rows, 1)
    scale = jnp.exp(own_top - joint_top) / joint_total

    no_tail = jnp.zeros((8, width), jnp.float32)
    residual, _ = scattered_sum(
        "pb",
        0,
        matmul(flipped[...], scale * target),
        no_tail,
        pb_out.at[0],
        pb_in.at[0],
        pb_all.at[0],
    )
    fitted = jnp.zeros_like(residual)
    direction = residual
    updates = None
    norm_now = None
    length_now = None
    for iteration in range(ITERS):
        forward = scale * matmul(kept_ref[...], residual)
        tail = tail_rows(column_sums(residual, residual), column_sums(residual, direction))
        summed, tail = scattered_sum(
            "ka",
            2 + 2 * iteration,
            forward,
            tail,
            ka_out.at[iteration],
            ka_in.at[iteration],
            ka_all.at[iteration],
        )
        norm_next = tail[0:1]
        if iteration == 0:
            updates = summed
            length_now = norm_next
        else:
            ratio = norm_next / norm_now
            direction = residual + ratio * direction
            updates = summed + ratio * updates
            length_now = norm_next + 2.0 * ratio * tail[1:2] + ratio * ratio * length_now
        norm_now = norm_next
        energy = tail_rows(column_sums(updates, updates))
        if iteration + 1 == ITERS:
            tail_out[...] = energy
            copies = begin("pb", 2 * ITERS, lambda peer: tail_out, tail_in.at[pb_me])
            tail_in[pb_me] = energy
            finish(copies)
            energy = tail_in[0]
            for source in range(1, pb_size):
                energy = energy + tail_in[source]
            step_length = norm_now / (energy[0:1] + ridge_weight * length_now)
            fitted_ref[...] = fitted + step_length * direction
        else:
            image, energy = scattered_sum(
                "pb",
                2 + 2 * iteration,
                matmul(flipped[...], scale * updates),
                energy,
                pb_out.at[iteration + 1],
                pb_in.at[iteration + 1],
                pb_all.at[iteration + 1],
            )
            step_length = norm_now / (energy[0:1] + ridge_weight * length_now)
            fitted = fitted + step_length * direction
            residual = residual - step_length * (image + ridge_weight * direction)


def fit(part, kept_exponent):
    ka_size, pb_size = lax.axis_size("ka"), lax.axis_size("pb")
    query_rows, kept_rows = kept_exponent.shape
    width = part.shape[1] // 2
    ka_share, pb_share = query_rows // ka_size, kept_rows // pb_size
    space = functools.partial(pltpu.VMEM, dtype=jnp.float32)
    return pl.pallas_call(
        functools.partial(fit_kernel, ka_size, pb_size),
        out_shape=jax.ShapeDtypeStruct((kept_rows, width), jnp.float32),
        in_specs=[pl.BlockSpec(memory_space=pltpu.VMEM)] * 2,
        out_specs=pl.BlockSpec(memory_space=pltpu.VMEM),
        scratch_shapes=[
            space((kept_rows, query_rows)),
            space((ka_size, ka_share, 2 * width)),
            space((ka_size, ka_share, 2 * width)),
            space((ITERS, ka_size, ka_share + 8, width)),
            space((ITERS, ka_size, ka_share + 8, width)),
            space((ITERS, ka_size, ka_share, width)),
            space((ITERS, pb_size, pb_share + 8, width)),
            space((ITERS, pb_size, pb_share + 8, width)),
            space((ITERS, pb_size, pb_share, width)),
            space((8, width)),
            space((pb_size, 8, width)),
            pltpu.SemaphoreType.DMA((2 + 2 * ITERS, ka_size)),
            pltpu.SemaphoreType.DMA((2 + 2 * ITERS, ka_size)),
            pltpu.SemaphoreType.DMA((2 * ITERS + 1, pb_size)),
            pltpu.SemaphoreType.DMA((2 * ITERS + 1, pb_size)),
        ],
        compiler_params=pltpu.CompilerParams(
            collective_id=0, has_side_effects=True, vmem_limit_bytes=40 * 1024 * 1024
        ),
    )(part.reshape(ka_size, ka_share, 2 * width), kept_exponent)


def thirds(value):
    first = value.astype(jnp.bfloat16)
    rest = value - first.astype(jnp.float32)
    second = rest.astype(jnp.bfloat16)
    third = (rest - second.astype(jnp.float32)).astype(jnp.bfloat16)
    return first, second, third


def target_kernel(inverse_root, queries_ref, keys_ref, values_ref, kept_ref, part_ref, wide, top, total, sums):
    width = queries_ref.shape[1]

    @pl.when(pl.program_id(0) == 0)
    def _():
        one, two, three = thirds(queries_ref[...])
        wide[...] = jnp.concatenate((one, one, two, one, three, two), axis=1)
        top[...] = jnp.full_like(top, -jnp.inf)
        total[...] = jnp.zeros_like(total)
        sums[...] = jnp.zeros_like(sums)

    one, two, three = thirds(keys_ref[...])
    scores = (
        lax.dot_general(
            wide[...],
            jnp.concatenate((one, two, one, three, one, two), axis=1),
            (((1,), (1,)), ((), ())),
            preferred_element_type=jnp.float32,
        )
        * inverse_root
    )
    top_next = jnp.maximum(top[...], jnp.max(scores, axis=1, keepdims=True))
    factor = jnp.exp(top[...] - top_next)
    exponent = jnp.exp(scores - top_next)
    top[...] = top_next
    total[...] = total[...] * factor + jnp.sum(exponent, axis=1, keepdims=True)
    one, two, three = thirds(values_ref[...])
    high, middle, low = thirds(exponent)
    pair = jnp.concatenate((one, two), axis=1)
    product = functools.partial(jnp.dot, preferred_element_type=jnp.float32)
    both = product(high, pair) + product(middle, pair)
    small = product(high, three) + product(low, one)
    sums[...] = sums[...] * factor + (both[:, :width] + (both[:, width:] + small))

    @pl.when(pl.program_id(0) == pl.num_programs(0) - 1)
    def _():
        lane = lax.broadcasted_iota(jnp.int32, kept_ref.shape, 1)
        stats = jnp.where(lane == 0, top[...], jnp.where(lane == 1, total[...], kept_ref[...]))
        part_ref[:, :width] = sums[...]
        part_ref[:, width:] = stats


def target_part(queries, cache_keys, cache_values, kept_stats, inverse_root):
    query_rows, width = queries.shape
    block_size = min(2048, cache_keys.shape[0])
    fixed = pl.BlockSpec((query_rows, width), lambda block: (0, 0))
    moving = pl.BlockSpec((block_size, width), lambda block: (block, 0))
    return pl.pallas_call(
        functools.partial(target_kernel, inverse_root),
        grid=(cache_keys.shape[0] // block_size,),
        out_shape=jax.ShapeDtypeStruct((query_rows, 2 * width), jnp.float32),
        in_specs=[fixed, moving, moving, fixed],
        out_specs=pl.BlockSpec((query_rows, 2 * width), lambda block: (0, 0)),
        scratch_shapes=[
            pltpu.VMEM((query_rows, 6 * width), jnp.bfloat16),
            pltpu.VMEM((query_rows, 1), jnp.float32),
            pltpu.VMEM((query_rows, 1), jnp.float32),
            pltpu.VMEM((query_rows, width), jnp.float32),
        ],
        compiler_params=pltpu.CompilerParams(vmem_limit_bytes=40 * 1024 * 1024),
    )(queries, cache_keys, cache_values, kept_stats)


def shards(queries, cache_keys, cache_values, kept_index):
    head_width = queries.shape[1]
    inverse_root = 1.0 / math.sqrt(head_width)
    cache_rows = cache_keys.shape[0]

    local_kept = kept_index - lax.axis_index("ka") * cache_rows
    kept_keys = jnp.take(cache_keys, local_kept, axis=0)
    kept_scores = contract(queries, kept_keys, 1, 1) * inverse_root
    kept_top = jnp.max(kept_scores, axis=1)
    kept_exponent = jnp.exp(kept_scores - kept_top[:, None])
    kept_total = jnp.sum(kept_exponent, axis=1)

    zero = jnp.zeros_like(kept_top)
    stats = jnp.stack((zero, zero, kept_top, kept_total), axis=1)
    stats = jnp.pad(stats, ((0, 0), (0, head_width - 4)))
    return fit(
        target_part(queries, cache_keys, cache_values, stats, inverse_root), kept_exponent
    )


def solution(mesh):
    in_specs = (P("pb", None), P("ka", None), P("ka", None), P("ka"))
    out_specs = P("ka", None)
    return jax.shard_map(shards, mesh=mesh, in_specs=in_specs, out_specs=out_specs, check_vma=False)
```
